512 devices in a mesh: bulk: 128 (over y, z, core), rep: 4 (over x).
Axes of the slice: x: 4, y: 8, z: 8, core: 2. Of those that a mesh axis runs over, the one named last changes fastest.
Arguments:
- orbitals: float32 [16384, 2048], P('rep', 'bulk'), may hold values from -6 to 6
- triangles: float32 [1024, 1024], P('rep', 'bulk'), may hold values from -0.09375 to 0.09375
- coupling: float32 [1024, 1024], P('rep', 'bulk'), may hold values from -0.09375 to 0.09375
- diagonals: float32 [2, 1024], P(None, 'bulk'), may hold values from 1 to 2
Outputs:
- solved: float32 [16384, 2048], P(('rep', 'bulk'))
The draws below stay inside these ranges and needn't reach their ends.
All inputs are finite; a program needn't handle non-finite values.
Results may differ from the reference program's by a relative error of at most 0.000084.
Values sent between devices are 32-bit elements; how exact they have to be, the bound alone decides.
A program may use at most 64 MiB of HBM per device.

```python
import jax
import jax.numpy as jnp
from jax import lax

PW = 1024
NB = 2048
COEF = 16384


def shard_levels(rng, dims, pieces, low, largest):
    factor_of = 1.0
    for axis_at, shards_of in pieces:
        heights = jax.random.uniform(jax.random.fold_in(jax.random.fold_in(rng, 6), axis_at), (shards_of,), jnp.float32, low / len(pieces), largest / len(pieces))
        factor_of = factor_of * jnp.repeat(jnp.exp(heights), dims[axis_at] // shards_of).reshape((-1,) + (1,) * (len(dims) - 1 - axis_at))
    return factor_of


def centred(own_key, extent, spread, bound, shards=(), held_as=jnp.bfloat16):
    level = shard_levels(own_key, extent, shards, -0.22, 0.18) if shards else 1.0
    values = jax.random.normal(own_key, extent, jnp.float32) * spread * level
    return jnp.minimum(jnp.maximum(values, -bound), bound).astype(held_as)


def setup_inputs(seed: int = 0) -> dict:
    arg_keys = jax.random.split(jax.random.key(seed), 5)
    orbitals = centred(arg_keys[0], (COEF, NB), 1.0, 6.0, ((0, 4), (1, 128)), jnp.float32)
    triangles = centred(arg_keys[1], (PW, PW), (4 * PW) ** -0.5, 0.09375, ((0, 4), (1, 128)), jnp.float32)
    coupling = centred(arg_keys[2], (PW, PW), (4 * PW) ** -0.5, 0.09375, ((0, 4), (1, 128)), jnp.float32)
    diagonals = jnp.clip(1.0 + 1.0 * jax.random.uniform(arg_keys[3], (2, PW), jnp.float32) ** shard_levels(arg_keys[3], (2, PW), ((1, 128),), -0.2, 0.2), 1.0, 2.0)
    return dict(orbitals=orbitals, triangles=triangles, coupling=coupling, diagonals=diagonals)


def unpack(triangles, diagonals):
    first_block = jnp.tril(triangles, -1) + jnp.diag(diagonals[0])
    second_block = jnp.tril(triangles.T, -1) + jnp.diag(diagonals[1])
    return (first_block, second_block)

def reference(orbitals, triangles, coupling, diagonals):
    first_block, second_block = unpack(triangles, diagonals)
    left_part = orbitals[:, :PW]
    right_part = orbitals[:, PW:]
    solved_one = jax.scipy.linalg.solve_triangular(first_block, left_part.T, lower=True).T
    update = jnp.dot(solved_one.astype(jnp.float32), coupling.T.astype(jnp.float32), precision=lax.Precision.HIGHEST, preferred_element_type=jnp.float32)
    solved_two = jax.scipy.linalg.solve_triangular(second_block, (right_part - update).T, lower=True).T
    return jnp.concatenate([solved_one, solved_two], axis=1)
```

```python
import functools

import jax
import jax.numpy as jnp
from jax import lax
from jax.experimental import pallas as pl
from jax.experimental.pallas import tpu as pltpu
from jax.sharding import PartitionSpec as P

F32 = jnp.float32
BF16 = jnp.bfloat16
BLK = 256
BASE = 16


def split(a):
    hi = a.astype(BF16)
    lo = (a - hi.astype(F32)).astype(BF16)
    return hi, lo


def dot(a, b, transposed=False):
    dims = (((1,), (1 if transposed else 0,)), ((), ()))
    return lax.dot_general(a, b, dims, preferred_element_type=F32)


def product(a, b):
    (ah, al), (bh, bl) = a, b
    return dot(ah, bh) + (dot(ah, bl) + dot(al, bh))


def thin_product(x, bh, bl, transposed=False):
    xh, xl = split(x)
    rows = x.shape[0]
    both = dot(jnp.concatenate([xh, xl], axis=0), bh, transposed)
    return both[:rows] + (both[rows:] + dot(xh, bl, transposed))


def unit_upper_inverses(mats):
    size = mats[0].shape[0]
    row = lax.broadcasted_iota(jnp.int32, (size, size), 0)
    col = lax.broadcasted_iota(jnp.int32, (size, size), 1)
    same = (row // BASE) == (col // BASE)
    power = [jnp.where(same, -n, 0.0) for n in mats]
    eye = jnp.where(row == col, 1.0, 0.0)
    inv = [eye + p for p in power]
    span = 2
    while span < BASE:
        power = [product(split(p), split(p)) for p in power]
        inv = [m + product(split(m), split(p)) for m, p in zip(inv, power)]
        span *= 2
    width = BASE
    while width < size:
        corner = ((row // width) % 2 == 0) & ((col // width) == (row // width) + 1)
        parts = [split(m) for m in inv]
        corners = [product(split(jnp.where(corner, n, 0.0)), m) for n, m in zip(mats, parts)]
        inv = [m - product(ms, split(c)) for m, ms, c in zip(inv, parts, corners)]
        width *= 2
    return inv


def solve_kernel(tri_ref, couple_ref, orb_ref, diag_ref, out_ref, mh_ref, ml_ref):
    panel = 1024
    count = panel // BLK
    row = lax.broadcasted_iota(jnp.int32, (BLK, BLK), 0)
    col = lax.broadcasted_iota(jnp.int32, (BLK, BLK), 1)
    upper = row < col

    for k in range(count):
        cut = pl.ds(BLK * k, BLK)
        block = tri_ref[k, cut, :]
        one = jnp.where(upper, block, 0.0) / diag_ref[0:1, cut]
        two = jnp.where(upper, block.T, 0.0) / diag_ref[1:2, cut]
        for which, m in enumerate(unit_upper_inverses([one, two])):
            mh_ref[which, k], ml_ref[which, k] = split(m)

    left = [orb_ref[:, pl.ds(BLK * k, BLK)] for k in range(count)]
    right = [orb_ref[:, pl.ds(panel + BLK * k, BLK)] for k in range(count)]
    for k in range(count):
        cut = pl.ds(BLK * k, BLK)
        x = thin_product(left[k] / diag_ref[0:1, cut], mh_ref[0, k], ml_ref[0, k])
        out_ref[:, cut] = x
        for i in range(k + 1, count):
            left[i] = left[i] - thin_product(x, *split(tri_ref[i, cut, :]))
        for i in range(count):
            right[i] = right[i] - thin_product(x, *split(couple_ref[i, cut, :]))
    for k in range(count):
        cut = pl.ds(BLK * k, BLK)
        x = thin_product(right[k] / diag_ref[1:2, cut], mh_ref[1, k], ml_ref[1, k])
        out_ref[:, pl.ds(panel + BLK * k, BLK)] = x
        for i in range(k + 1, count):
            tri = tri_ref[k, pl.ds(BLK * i, BLK), :]
            right[i] = right[i] - thin_product(x, *split(tri), transposed=True)


def solve(tri, couple, orb, diag):
    rows = orb.shape[0]
    vmem = pl.BlockSpec(memory_space=pltpu.VMEM)
    return pl.pallas_call(
        solve_kernel,
        out_shape=jax.ShapeDtypeStruct((rows, 2048), F32),
        in_specs=[vmem] * 4,
        out_specs=vmem,
        scratch_shapes=[pltpu.VMEM((2, 4, BLK, BLK), BF16), pltpu.VMEM((2, 4, BLK, BLK), BF16)],
        compiler_params=pltpu.CompilerParams(vmem_limit_bytes=48 << 20),
        name="solve",
    )(tri, couple, orb, diag)


def per_device(orbitals, triangles, coupling, diagonals):
    groups = lax.axis_size("bulk")
    diag_rows = jnp.pad(diagonals, ((0, 6), (0, 248)))
    mine = jnp.concatenate([triangles.T, coupling.T, diag_rows], axis=0)
    whole = lax.all_gather(mine, ("rep", "bulk"))
    whole = whole.reshape(4, groups, 24, 256)
    tri = whole[:, :, 0:8].reshape(4, 1024, 256)
    couple = whole[:, :, 8:16].reshape(4, 1024, 256)
    diag = whole[0, :, 16:18, 0:8].transpose(1, 0, 2).reshape(2, 1024)
    local_rows = orbitals.shape[0] // groups
    blocks = orbitals.reshape(groups, local_rows, orbitals.shape[1])
    received = lax.all_to_all(blocks, "bulk", split_axis=0, concat_axis=2, tiled=True)
    orb = received.reshape(local_rows, 2048)
    return solve(tri, couple, orb, diag)


def solution(mesh):
    return jax.shard_map(
        per_device,
        mesh=mesh,
        in_specs=(P("rep", "bulk"), P("rep", "bulk"), P("rep", "bulk"), P(None, "bulk")),
        out_specs=P(("rep", "bulk"), None),
        check_vma=False,
    )
```

```python
import functools

import jax
import jax.numpy as jnp
from jax import lax
from jax.experimental import pallas as pl
from jax.experimental.pallas import tpu as pltpu
from jax.sharding import PartitionSpec as P

F32 = jnp.float32
BF16 = jnp.bfloat16
BLK = 256
BASE = 16
MESH = pl.DeviceIdType.MESH
NX, NY, NZ = 4, 8, 8
COPIES = 320


def split(a):
    hi = a.astype(BF16)
    lo = (a - hi.astype(F32)).astype(BF16)
    return hi, lo


def dot(a, b, transposed=False):
    dims = (((1,), (1 if transposed else 0,)), ((), ()))
    return lax.dot_general(a, b, dims, preferred_element_type=F32)


def product(a, b):
    (ah, al), (bh, bl) = a, b
    return dot(ah, bh) + (dot(ah, bl) + dot(al, bh))


def thin_product(x, bh, bl, transposed=False):
    xh, xl = split(x)
    rows = x.shape[0]
    both = dot(jnp.concatenate([xh, xl], axis=0), bh, transposed)
    return both[:rows] + (both[rows:] + dot(xh, bl, transposed))


def unit_upper_inverses(mats):
    size = mats[0].shape[0]
    row = lax.broadcasted_iota(jnp.int32, (size, size), 0)
    col = lax.broadcasted_iota(jnp.int32, (size, size), 1)
    same = (row // BASE) == (col // BASE)
    power = [jnp.where(same, -n, 0.0) for n in mats]
    eye = jnp.where(row == col, 1.0, 0.0)
    inv = [eye + p for p in power]
    span = 2
    while span < BASE:
        power = [product(split(p), split(p)) for p in power]
        inv = [m + product(split(m), split(p)) for m, p in zip(inv, power)]
        span *= 2
    width = BASE
    while width < size:
        corner = ((row // width) % 2 == 0) & ((col // width) == (row // width) + 1)
        parts = [split(m) for m in inv]
        corners = [product(split(jnp.where(corner, n, 0.0)), m) for n, m in zip(mats, parts)]
        inv = [m - product(ms, split(c)) for m, ms, c in zip(inv, parts, corners)]
        width *= 2
    return inv


def pack_kernel(orb_ref, tri_ref, couple_ref, diag_ref, mine_ref, diag_tile_ref, sent_ref):
    for half in range(2):
        cut = pl.ds(128 * half, 128)
        mine_ref[0, half] = tri_ref[:, cut]
        mine_ref[1, half] = couple_ref[:, cut]
    place = lax.axis_index("bulk") % 16
    lane = lax.broadcasted_iota(jnp.int32, (2, 128), 1)
    spread = jnp.concatenate([diag_ref[...]] * 16, axis=1)
    diag_tile_ref[...] = jnp.where(lane // 8 == place, spread, 0.0)
    group = lax.broadcasted_iota(jnp.int32, (8, 128), 1) // 16
    for g in range(4):
        stack = jnp.concatenate([orb_ref[:, pl.ds(128 * (8 * g + t), 128)] for t in range(8)], axis=0)
        turned = stack.T
        for p in range(2):
            pieces = [turned[64 * p + 8 * h : 64 * p + 8 * h + 8] for h in range(8)]
            for t in range(8):
                tile = jnp.zeros((8, 128), F32)
                for h in range(8):
                    moved = pieces[h] if h == t else pltpu.roll(pieces[h], (16 * (h - t)) % 128, 1)
                    tile = jnp.where(group == h, moved, tile)
                sent_ref[2 * (8 * g + t) + p] = tile


def pack(orbitals, triangles, coupling, diagonals):
    vmem = pl.BlockSpec(memory_space=pltpu.VMEM)
    return pl.pallas_call(
        pack_kernel,
        out_shape=(
            jax.ShapeDtypeStruct((2, 2, 8, 128), F32),
            jax.ShapeDtypeStruct((2, 128), F32),
            jax.ShapeDtypeStruct((NY * NZ, 8, 128), F32),
        ),
        in_specs=[vmem] * 4,
        out_specs=(vmem,) * 3,
        name="pack",
    )(orbitals, triangles, coupling, diagonals)


def ring_hops(n):
    return [(1, d) for d in range(1, n // 2 + 1)] + [(-1, d) for d in range(1, n - n // 2)]


class Copies:
    def __init__(self, send, recv):
        self.send, self.recv, self.count, self.started = send, recv, 0, []

    def slot(self):
        self.count += 1
        return self.count - 1

    def remote(self, src, dst, device):
        at = self.slot()
        copy = pltpu.make_async_remote_copy(
            src_ref=src, dst_ref=dst, send_sem=self.send.at[at], recv_sem=self.recv.at[at],
            device_id=device, device_id_type=MESH)
        copy.start()
        self.started.append(copy)
        return copy


def exchange_kernel(mine, diag_tile, sent, whole, diags, orbs, first, local, send, recv):
    bulk, x = lax.axis_index("bulk"), lax.axis_index("rep")
    c = lax.rem(bulk, 2)
    z = lax.rem(bulk // 2, NZ)
    y = bulk // (2 * NZ)
    s = 1 - 2 * c
    me = {"x": x, "y": y, "z": z}
    size = {"x": NX, "y": NY, "z": NZ}

    def shifted(axis, by):
        return lax.rem(me[axis] + by + 2 * size[axis], size[axis])

    def device(axis, by):
        at = dict(me)
        at[axis] = shifted(axis, by)
        return ((at["y"] * NZ + at["z"]) * 2 + c, at["x"])

    partner = (bulk + s, x)
    barrier = pltpu.get_barrier_semaphore()
    peers = [device(a, o) for a in "xyz" for o in range(1, size[a])] + [partner]
    for peer in peers:
        pl.semaphore_signal(barrier, inc=1, device_id=peer, device_id_type=MESH)
    pl.semaphore_wait(barrier, len(peers))

    copies = Copies(send, recv)
    keep = pltpu.make_async_copy(mine, whole.at[:, :, x, y, z, c], local.at[0])
    keep_diag = pltpu.make_async_copy(diag_tile, diags.at[y, z, c], local.at[1])
    keep_first = pltpu.make_async_copy(sent.at[y], first.at[y], local.at[2])
    for copy in (keep, keep_diag, keep_first):
        copy.start()

    lines = []
    for o in range(1, 8):
        for half, axis in ((0, "z"), (1, "y")):
            lines.append(copies.remote(mine.at[:, half], whole.at[:, half, x, y, z, c], device(axis, o)))
    diag_line = [copies.remote(diag_tile, diags.at[y, z, c], device("z", o)) for o in range(1, 8)]

    colours = [(1, 0, "z", "y", "x"), (1, 1, "y", "z", "x"), (0, 0, "z", "x", "y"), (0, 1, "y", "x", "z")]

    def block(colour, index):
        t, half, line, _, _ = colour
        at = {**me, **index}
        at[line] = slice(None)
        return whole.at[t, half, at["x"], at["y"], at["z"], c]

    events = {}

    def later(slot, action):
        events.setdefault(slot, []).append(action)

    def to_partner(ref):
        crossing.append(copies.remote(ref, ref, partner))

    crossing = []

    def start_ring(colour, axis, index, slot, arrived):
        n = size[axis]
        hops = ring_hops(n)
        own = block(colour, {**index, axis: me[axis]})
        coming = {}
        for way in (1, -1):
            coming[way, 1] = copies.remote(own, own, device(axis, way * s))
        for way, d in sorted(hops, key=lambda h: h[1]):
            def action(way=way, d=d):
                coming[way, d].wait_recv()
                at = shifted(axis, -way * s * d)
                ref = block(colour, {**index, axis: at})
                if (way, d + 1) in hops:
                    coming[way, d + 1] = copies.remote(ref, ref, device(axis, way * s))
                arrived(axis, at, slot + d)
            later(slot + d, action)

    def final_arrival(colour, index):
        def arrived(axis, at, slot):
            to_partner(block(colour, {**index, axis: at}))
        return arrived

    def middle_arrival(colour):
        def arrived(axis, at, slot):
            start_ring(colour, colour[4], {axis: at}, slot, final_arrival(colour, {axis: at}))
            to_partner(block(colour, {axis: at}))
        return arrived

    for copy in lines:
        copy.wait_recv()
    keep.wait()
    for colour in colours:
        start_ring(colour, colour[3], {}, 0, middle_arrival(colour))
    for colour in colours:
        start_ring(colour, colour[4], {}, 0, final_arrival(colour, {}))
    for colour in colours:
        to_partner(block(colour, {}))

    keep_first.wait()
    turned = [copies.remote(sent.at[shifted("y", o)], first.at[y], device("y", o)) for o in range(1, 8)]

    def diag_second():
        for copy in diag_line:
            copy.wait_recv()
        keep_diag.wait()
        diag_blocks.extend(
            copies.remote(diags.at[y, :, c], diags.at[y, :, c], device("y", o)) for o in range(1, 8))

    def orbital_second():
        for copy in turned:
            copy.wait_recv()
        keep_second = pltpu.make_async_copy(first.at[:, z], orbs.at[c, z], local.at[3])
        keep_second.start()
        orbital_blocks.extend(
            copies.remote(first.at[:, shifted("z", o)], orbs.at[c, z], device("z", o)) for o in range(1, 8))
        keep_second.wait()

    def diag_last():
        for copy in diag_blocks:
            copy.wait_recv()
        to_partner(diags.at[:, :, c])

    def orbital_last():
        for copy in orbital_blocks:
            copy.wait_recv()
        to_partner(orbs.at[c])

    diag_blocks, orbital_blocks = [], []
    later(1, diag_second)
    later(2, orbital_second)
    later(3, diag_last)
    later(5, orbital_last)
    slot = 0
    while slot <= max(events):
        for action in events.get(slot, []):
            action()
        slot += 1
    for copy in crossing:
        copy.wait_recv()
    for copy in copies.started:
        copy.wait_send()


def exchange(mine, diag_tile, sent):
    anywhere = pl.BlockSpec(memory_space=pl.ANY)
    vmem = pl.BlockSpec(memory_space=pltpu.VMEM)
    return pl.pallas_call(
        exchange_kernel,
        out_shape=(
            jax.ShapeDtypeStruct((2, 2, NX, NY, NZ, 2, 8, 128), F32),
            jax.ShapeDtypeStruct((NY, NZ, 2, 2, 128), F32),
            jax.ShapeDtypeStruct((2, NZ, NY, 8, 128), F32),
        ),
        in_specs=[vmem] * 3,
        out_specs=(anywhere,) * 3,
        scratch_shapes=[
            pltpu.VMEM((NY, NZ, 8, 128), F32),
            pltpu.SemaphoreType.DMA((4,)),
            pltpu.SemaphoreType.DMA((COPIES,)),
            pltpu.SemaphoreType.DMA((COPIES,)),
        ],
        compiler_params=pltpu.CompilerParams(collective_id=0, has_side_effects=True),
        name="exchange",
    )(mine, diag_tile, sent.reshape(NY, NZ, 8, 128))


def solve_kernel(whole_ref, diags_ref, orbs_ref, out_ref, mh_ref, ml_ref):
    panel = 1024
    count = panel // BLK
    row = lax.broadcasted_iota(jnp.int32, (BLK, BLK), 0)
    col = lax.broadcasted_iota(jnp.int32, (BLK, BLK), 1)
    upper = row < col

    def factor(t, i, j):
        cut = pl.ds(BLK * j, BLK)
        return jnp.concatenate([whole_ref[t, 0, i, cut, :], whole_ref[t, 1, i, cut, :]], axis=1)

    scales = []
    for which in range(2):
        rows = [jnp.sum(diags_ref[w, :, which, :], axis=0, keepdims=True) for w in range(8)]
        scales.append([1.0 / jnp.concatenate(rows[2 * k : 2 * k + 2], axis=1) for k in range(count)])

    for k in range(count):
        block = factor(0, k, k)
        one = jnp.where(upper, block, 0.0) * scales[0][k]
        two = jnp.where(upper, block.T, 0.0) * scales[1][k]
        for which, m in enumerate(unit_upper_inverses([one, two])):
            mh_ref[which, k], ml_ref[which, k] = split(m)

    odd = lax.axis_index("bulk") % 2 == 1
    group = lax.broadcasted_iota(jnp.int32, (8, 128), 1) // 16
    columns = []
    for w in range(16):
        tiles = [orbs_ref[e % 2, 4 * (w % 2) + e // 2, w // 2] for e in range(8)]
        tiles = [jnp.where(odd, pltpu.roll(t, 64, 1), t) for t in tiles]
        strips = []
        for h in range(4):
            strip = jnp.zeros((8, 128), F32)
            for e in range(8):
                moved = tiles[e] if e == h else pltpu.roll(tiles[e], (16 * (e - h)) % 128, 1)
                strip = jnp.where(group == e, moved, strip)
            strips.append(strip)
        columns.append(jnp.concatenate(strips, axis=0))
    blocks = [jnp.concatenate(columns[2 * k : 2 * k + 2], axis=1) for k in range(2 * count)]
    left, right = blocks[:count], blocks[count:]

    for k in range(count):
        x = thin_product(left[k] * scales[0][k], mh_ref[0, k], ml_ref[0, k])
        out_ref[:, pl.ds(BLK * k, BLK)] = x
        for i in range(k + 1, count):
            left[i] = left[i] - thin_product(x, *split(factor(0, i, k)))
        for i in range(count):
            right[i] = right[i] - thin_product(x, *split(factor(1, i, k)))
    for k in range(count):
        x = thin_product(right[k] * scales[1][k], mh_ref[1, k], ml_ref[1, k])
        out_ref[:, pl.ds(panel + BLK * k, BLK)] = x
        for i in range(k + 1, count):
            right[i] = right[i] - thin_product(x, *split(factor(0, k, i)), transposed=True)


def solve(whole, diags, orbs):
    vmem = pl.BlockSpec(memory_space=pltpu.VMEM)
    return pl.pallas_call(
        solve_kernel,
        out_shape=jax.ShapeDtypeStruct((32, 2048), F32),
        in_specs=[vmem] * 3,
        out_specs=vmem,
        scratch_shapes=[pltpu.VMEM((2, 4, BLK, BLK), BF16), pltpu.VMEM((2, 4, BLK, BLK), BF16)],
        compiler_params=pltpu.CompilerParams(vmem_limit_bytes=32 << 20),
        name="solve",
    )(whole.reshape(2, 2, NX, 1024, 128), diags.reshape(8, 16, 2, 128), orbs)


def per_device(orbitals, triangles, coupling, diagonals):
    mine, diag_tile, sent = pack(orbitals.T, triangles.T, coupling.T, diagonals)
    return solve(*exchange(mine, diag_tile, sent))


def solution(mesh):
    return jax.shard_map(
        per_device,
        mesh=mesh,
        in_specs=(P("rep", "bulk"), P("rep", "bulk"), P("rep", "bulk"), P(None, "bulk")),
        out_specs=P(("rep", "bulk"), None),
        check_vma=False,
    )
```

```python
import functools

import jax
import jax.numpy as jnp
from jax import lax
from jax.experimental import pallas as pl
from jax.experimental.pallas import tpu as pltpu
from jax.sharding import PartitionSpec as P

F32 = jnp.float32
BF16 = jnp.bfloat16
BLK = 256
BASE = 16
MESH = pl.DeviceIdType.MESH
NX, NY, NZ = 4, 8, 8
COPIES = 320


def split(a):
    hi = a.astype(BF16)
    lo = (a - hi.astype(F32)).astype(BF16)
    return hi, lo


def dot(a, b, transposed=False):
    dims = (((1,), (1 if transposed else 0,)), ((), ()))
    return lax.dot_general(a, b, dims, preferred_element_type=F32)


def product(a, b):
    (ah, al), (bh, bl) = a, b
    return dot(ah, bh) + (dot(ah, bl) + dot(al, bh))


def thin_product(x, bh, bl, transposed=False):
    xh, xl = split(x)
    rows = x.shape[0]
    both = dot(jnp.concatenate([xh, xl], axis=0), bh, transposed)
    return both[:rows] + (both[rows:] + dot(xh, bl, transposed))


def unit_upper_inverses(mats):
    size = mats[0].shape[0]
    row = lax.broadcasted_iota(jnp.int32, (size, size), 0)
    col = lax.broadcasted_iota(jnp.int32, (size, size), 1)
    same = (row // BASE) == (col // BASE)
    eye = jnp.where(row == col, 1.0, 0.0)
    power = [jnp.where(same, -n, 0.0) for n in mats]
    inv = [eye + p for p in power]
    span = 2
    while span < BASE:
        parts = [split(p) for p in power]
        power = [product(p, p) for p in parts]
        parts = [split(p) for p in power]
        inv = [m + product(split(m), p) for m, p in zip(inv, parts)]
        span *= 2
    width = BASE
    while width < size:
        corner = ((row // width) % 2 == 0) & ((col // width) == (row // width) + 1)
        parts = [split(m) for m in inv]
        corners = [product(split(jnp.where(corner, n, 0.0)), m) for n, m in zip(mats, parts)]
        inv = [m - product(ms, split(c)) for m, ms, c in zip(inv, parts, corners)]
        width *= 2
    return [split(m) for m in inv]


def ring_hops(n):
    return [(1, d) for d in range(1, n // 2 + 1)] + [(-1, d) for d in range(1, n - n // 2)]


def exchange_body(tri, couple, orb, diag, whole, diags, orbs, sent, first, diag_tile, diag_in, orb_in, local, send, recv, pack_work, invert, unpack):
    bulk, x = lax.axis_index("bulk"), lax.axis_index("rep")
    c = lax.rem(bulk, 2)
    z = lax.rem(bulk // 2, NZ)
    y = bulk // (2 * NZ)
    s = 1 - 2 * c
    me = {"x": x, "y": y, "z": z}
    size = {"x": NX, "y": NY, "z": NZ}
    used = {"send": 0, "recv": 0}

    def new(kind):
        used[kind] += 1
        return used[kind] - 1

    def shifted(axis, by):
        return lax.rem(me[axis] + by + 2 * size[axis], size[axis])

    def device(axis, by):
        at = dict(me)
        at[axis] = shifted(axis, by)
        return ((at["y"] * NZ + at["z"]) * 2 + c, at["x"])

    partner = (bulk + s, x)

    def put(src, dst, to, send_at, recv_at):
        pltpu.make_async_remote_copy(
            src_ref=src, dst_ref=dst, send_sem=send.at[send_at], recv_sem=recv.at[recv_at],
            device_id=to, device_id_type=MESH).start()

    def take(sem, ref):
        pltpu.make_async_copy(ref, ref, sem).wait()

    get_diag = pltpu.make_async_copy(diag, diag_in, local.at[0])
    get_orb = pltpu.make_async_copy(orb, orb_in, local.at[1])
    get_orb.start()
    get_diag.start()
    barrier = pltpu.get_barrier_semaphore()
    peers = [device(a, o) for a in "xyz" for o in range(1, size[a])] + [partner]
    for peer in peers:
        pl.semaphore_signal(barrier, inc=1, device_id=peer, device_id_type=MESH)
    keeps = []
    for t, ref in ((0, tri), (1, couple)):
        for half in range(2):
            keep = pltpu.make_async_copy(ref.at[:, pl.ds(128 * half, 128)], whole.at[t, half, x, y, z, c], local.at[2 + 2 * t + half])
            keep.start()
            keeps.append(keep)
    pl.semaphore_wait(barrier, len(peers))

    line_send = new("send")
    line_recv = {(t, half): new("recv") for t in range(2) for half in range(2)}
    order = (4, 3, 5, 2, 6, 1, 7)
    for t, ref in ((1, couple), (0, tri)):
        for o in order:
            for half, axis in ((0, "z"), (1, "y")):
                put(ref.at[:, pl.ds(128 * half, 128)], whole.at[t, half, x, y, z, c], device(axis, o), line_send, line_recv[t, half])

    pack_work(get_orb, get_diag)
    put_diag = pltpu.make_async_copy(diag_tile, diags.at[y, z, c], local.at[6])
    put_diag.start()
    keep_first = pltpu.make_async_copy(sent.at[y], first.at[y], local.at[7])
    keep_first.start()
    diag_send, diag_recv = new("send"), new("recv")
    for o in order:
        put(diag_tile, diags.at[y, z, c], device("z", o), diag_send, diag_recv)

    colours = [(1, 0, "z", "y", "x"), (1, 1, "y", "z", "x"), (0, 0, "z", "x", "y"), (0, 1, "y", "x", "z")]
    ring_send = {colour: (new("send"), new("send")) for colour in colours}
    cross_send = new("send")
    cross_recv = {colour: new("recv") for colour in colours}

    def block(colour, index):
        t, half, line, _, _ = colour
        at = {**me, **index}
        at[line] = slice(None)
        return whole.at[t, half, at["x"], at["y"], at["z"], c]

    def blocks_like(n):
        a = {1: (1, 1), 2: (2, 1), 7: (1, 7), 3: (3, 1), 24: (3, 8), 28: (4, 7), 32: (4, 8)}[n]
        return whole.at[0, 0, pl.ds(0, a[0]), pl.ds(0, a[1]), :, 0]

    events = {}

    def later(slot, action, rank=0):
        events.setdefault(slot, []).append((rank, len(events.get(slot, [])), action))

    crossings = []

    def to_partner(colour, ref):
        put(ref, ref, partner, cross_send, cross_recv[colour])
        crossings.append(colour)

    def final_ring(colour, indices, slot):
        axis = colour[4]
        n, hops = size[axis], ring_hops(size[axis])
        sems = {hop: new("recv") for hop in hops}
        for index in indices:
            own = block(colour, index)
            for way in (1, -1):
                put(own, own, device(axis, way * s), ring_send[colour][1], sems[way, 1])
            to_partner(colour, own)
        for way, d in sorted(hops, key=lambda h: h[1]):
            def action(way=way, d=d):
                take(recv.at[sems[way, d]], blocks_like(len(indices)))
                for index in indices:
                    ref = block(colour, {**index, axis: shifted(axis, -way * s * d)})
                    if (way, d + 1) in hops:
                        put(ref, ref, device(axis, way * s), ring_send[colour][1], sems[way, d + 1])
                    to_partner(colour, ref)
            later(slot + d, action, 1)

    def middle_ring(colour):
        axis = colour[3]
        n, hops = size[axis], ring_hops(size[axis])
        sems = {hop: new("recv") for hop in hops}
        own = block(colour, {})
        for way in (1, -1):
            put(own, own, device(axis, way * s), ring_send[colour][0], sems[way, 1])
        for d in range(1, n // 2 + 1):
            ways = [way for way in (1, -1) if (way, d) in hops]
            def action(d=d, ways=ways):
                indices = []
                for way in ways:
                    take(recv.at[sems[way, d]], blocks_like(1))
                    index = {axis: shifted(axis, -way * s * d)}
                    ref = block(colour, index)
                    if (way, d + 1) in hops:
                        put(ref, ref, device(axis, way * s), ring_send[colour][0], sems[way, d + 1])
                    indices.append(index)
                final_ring(colour, indices, d)
            later(d, action)

    for keep in keeps:
        keep.wait()
    for colour in colours:
        take(recv.at[line_recv[colour[0], colour[1]]], whole.at[0, 0, 0, 0, pl.ds(0, 7), 0])
        middle_ring(colour)
    for colour in colours:
        final_ring(colour, [{}], 0)

    first_send, first_recv, second_send, second_recv = new("send"), new("recv"), new("send"), new("recv")
    dblock_send, dblock_recv = new("send"), new("recv")
    cross_small = [(new("send"), new("recv")) for _ in range(2)]

    def orbital_first():
        keep_first.wait()
        for o in order:
            at = shifted("y", o)
            put(sent.at[at], first.at[y], device("y", o), first_send, first_recv)

    def orbital_second():
        take(recv.at[first_recv], first.at[pl.ds(0, 7)])
        keep_second = pltpu.make_async_copy(first.at[:, z], orbs.at[c, z], local.at[8])
        keep_second.start()
        for o in order:
            put(first.at[:, shifted("z", o)], orbs.at[c, z], device("z", o), second_send, second_recv)
        keep_second.wait()

    def orbital_last():
        take(recv.at[second_recv], orbs.at[0, pl.ds(0, 7)])
        put(orbs.at[c], orbs.at[c], partner, *cross_small[0])

    def diag_second():
        put_diag.wait()
        take(recv.at[diag_recv], diags.at[0, pl.ds(0, 7), 0])
        for o in order:
            put(diags.at[y, :, c], diags.at[y, :, c], device("y", o), dblock_send, dblock_recv)

    def diag_last():
        take(recv.at[dblock_recv], diags.at[pl.ds(0, 7), :, 0])
        put(diags.at[:, :, c], diags.at[:, :, c], partner, *cross_small[1])

    later(0, orbital_first, 2)
    later(2, orbital_second, 2)
    later(5, orbital_last, 2)
    later(1, diag_second, 2)
    later(3, diag_last, 2)
    def triangles_ready():
        take(recv.at[cross_small[1][1]], diags.at[:, :, 0])
        for colour in colours[2:]:
            take(recv.at[cross_recv[colour]], blocks_like(32))
        invert()

    def orbitals_ready():
        take(recv.at[cross_small[0][1]], orbs.at[0])
        unpack()

    later(6, triangles_ready, 5)
    later(6, orbitals_ready, 6)
    slot = 0
    while slot <= max(events):
        done = 0
        while done < len(events.get(slot, [])):
            todo = sorted(events[slot][done:])
            done += len(todo)
            for _, _, action in todo:
                action()
        slot += 1

    for colour in colours[:2]:
        take(recv.at[cross_recv[colour]], blocks_like(32))

    def finish():
        take(send.at[line_send], whole.at[:, :, 0, 0, pl.ds(0, 7), 0])
        take(send.at[diag_send], diags.at[0, pl.ds(0, 7), 0])
        for colour in colours:
            take(send.at[ring_send[colour][0]], blocks_like(7 if size[colour[3]] == 8 else 3))
            take(send.at[ring_send[colour][1]], blocks_like(24 if size[colour[4]] == 4 else 28))
        take(send.at[cross_send], whole.at[:, :, :, :, :, 0])
        take(send.at[first_send], first.at[pl.ds(0, 7)])
        take(send.at[second_send], orbs.at[0, pl.ds(0, 7)])
        take(send.at[dblock_send], diags.at[pl.ds(0, 7), :, 0])
        take(send.at[cross_small[0][0]], orbs.at[0])
        take(send.at[cross_small[1][0]], diags.at[:, :, 0])

    assert used["send"] <= SENDS and used["recv"] <= RECVS, used
    return finish


def pack_into(orb_in, diag_in, sent, diag_tile):
    place = lax.axis_index("bulk") % 16
    lane = lax.broadcasted_iota(jnp.int32, (2, 128), 1)
    spread = jnp.concatenate([diag_in[...]] * 16, axis=1)
    diag_tile[...] = jnp.where(lane // 8 == place, spread, 0.0)
    group = lax.broadcasted_iota(jnp.int32, (8, 128), 1) // 16
    for g in range(4):
        stack = jnp.concatenate([orb_in[:, pl.ds(128 * (8 * g + t), 128)] for t in range(8)], axis=0)
        turned = stack.T
        for p in range(2):
            pieces = [turned[64 * p + 8 * h : 64 * p + 8 * h + 8] for h in range(8)]
            for t in range(8):
                tile = jnp.zeros((8, 128), F32)
                for h in range(8):
                    moved = pieces[h] if h == t else pltpu.roll(pieces[h], (16 * (h - t)) % 128, 1)
                    tile = jnp.where(group == h, moved, tile)
                chip = 2 * (8 * g + t) + p
                sent[chip // NZ, chip % NZ] = tile


def exchange_kernel(tri, couple, orb, diag, out_ref, whole, diags, orbs, sent, first, diag_tile, diag_in, orb_in, mh_ref, ml_ref, local, send, recv):
    def pack_work(get_orb, get_diag):
        get_diag.wait()
        get_orb.wait()
        pack_into(orb_in, diag_in, sent, diag_tile)

    panel = 1024
    count = panel // BLK
    row = lax.broadcasted_iota(jnp.int32, (BLK, BLK), 0)
    col = lax.broadcasted_iota(jnp.int32, (BLK, BLK), 1)
    upper = row < col

    def factor(t, i, j):
        return jnp.concatenate([whole[t, half, i, 2 * j : 2 * j + 2].reshape(BLK, 128) for half in range(2)], axis=1)

    state = {}

    def invert():
        scales = []
        for which in range(2):
            rows = [jnp.sum(diags[w, :, :, which, :].reshape(16, 128), axis=0, keepdims=True) for w in range(8)]
            scales.append([1.0 / jnp.concatenate(rows[2 * k : 2 * k + 2], axis=1) for k in range(count)])

        half = BLK // 2
        above = upper[:half, :half]
        mats, corners = [], []
        for k in range(count):
            block = factor(0, k, k)
            for which, turned in ((0, block), (1, block.T)):
                scaled = turned * scales[which][k]
                mats += [jnp.where(above, scaled[:half, :half], 0.0), jnp.where(above, scaled[half:, half:], 0.0)]
                corners.append(scaled[:half, half:])
        invs = unit_upper_inverses(mats)
        inner = [product(split(n), invs[2 * e + 1]) for e, n in enumerate(corners)]
        inner = [split(-product(invs[2 * e], split(n))) for e, n in enumerate(inner)]
        for k in range(count):
            for which in range(2):
                e = 2 * k + which
                for at, ref in enumerate((mh_ref, ml_ref)):
                    ref[which, k, :half, :half] = invs[2 * e][at]
                    ref[which, k, half:, half:] = invs[2 * e + 1][at]
                    ref[which, k, :half, half:] = inner[e][at]
                    ref[which, k, half:, :half] = jnp.zeros((half, half), BF16)

        state["scales"] = scales

    def unpack():
        odd = lax.axis_index("bulk") % 2 == 1
        group = lax.broadcasted_iota(jnp.int32, (8, 128), 1) // 16
        columns = []
        for w in range(16):
            tiles = [orbs[e % 2, 4 * (w % 2) + e // 2, w // 2] for e in range(8)]
            tiles = [jnp.where(odd, pltpu.roll(t, 64, 1), t) for t in tiles]
            strips = []
            for h in range(4):
                strip = jnp.zeros((8, 128), F32)
                for e in range(8):
                    moved = tiles[e] if e == h else pltpu.roll(tiles[e], (16 * (e - h)) % 128, 1)
                    strip = jnp.where(group == e, moved, strip)
                strips.append(strip)
            columns.append(jnp.concatenate(strips, axis=0))
        blocks = [jnp.concatenate(columns[2 * k : 2 * k + 2], axis=1) for k in range(2 * count)]
        left, right = blocks[:count], blocks[count:]
        state["columns"] = left, right

    finish = exchange_body(tri, couple, orb, diag, whole, diags, orbs, sent, first, diag_tile, diag_in, orb_in, local, send, recv, pack_work, invert, unpack)
    scales = state["scales"]
    left, right = state["columns"]
    for k in range(count):
        x = thin_product(left[k] * scales[0][k], mh_ref[0, k], ml_ref[0, k])
        out_ref[:, pl.ds(BLK * k, BLK)] = x
        for i in range(k + 1, count):
            left[i] = left[i] - thin_product(x, *split(factor(0, i, k)))
        for i in range(count):
            right[i] = right[i] - thin_product(x, *split(factor(1, i, k)))
    for k in range(count):
        x = thin_product(right[k] * scales[1][k], mh_ref[1, k], ml_ref[1, k])
        out_ref[:, pl.ds(panel + BLK * k, BLK)] = x
        for i in range(k + 1, count):
            right[i] = right[i] - thin_product(x, *split(factor(0, k, i)), transposed=True)


    finish()


SENDS, RECVS = 24, 110


def exchange(orbitals, triangles, coupling, diagonals):
    anywhere = pl.BlockSpec(memory_space=pl.ANY)
    vmem = pl.BlockSpec(memory_space=pltpu.VMEM)
    return pl.pallas_call(
        exchange_kernel,
        out_shape=jax.ShapeDtypeStruct((32, 2048), F32),
        in_specs=[anywhere] * 4,
        out_specs=vmem,
        scratch_shapes=[
            pltpu.VMEM((2, 2, NX, NY, NZ, 2, 8, 128), F32),
            pltpu.VMEM((NY, NZ, 2, 2, 128), F32),
            pltpu.VMEM((2, NZ, NY, 8, 128), F32),
            pltpu.VMEM((NY, NZ, 8, 128), F32),
            pltpu.VMEM((NY, NZ, 8, 128), F32),
            pltpu.VMEM((2, 128), F32),
            pltpu.VMEM((2, 8), F32),
            pltpu.VMEM((16, 4096), F32),
            pltpu.VMEM((2, 4, BLK, BLK), BF16),
            pltpu.VMEM((2, 4, BLK, BLK), BF16),
            pltpu.SemaphoreType.DMA((9,)),
            pltpu.SemaphoreType.DMA((SENDS,)),
            pltpu.SemaphoreType.DMA((RECVS,)),
        ],
        compiler_params=pltpu.CompilerParams(collective_id=0, has_side_effects=True, vmem_limit_bytes=62 << 20),
        name="exchange",
    )(triangles, coupling, orbitals, diagonals)


def per_device(orbitals, triangles, coupling, diagonals):
    return exchange(orbitals.T, triangles.T, coupling.T, diagonals)


def solution(mesh):
    return jax.shard_map(
        per_device,
        mesh=mesh,
        in_specs=(P("rep", "bulk"), P("rep", "bulk"), P("rep", "bulk"), P(None, "bulk")),
        out_specs=P(("rep", "bulk"), None),
        check_vma=False,
    )
```

```python
import functools
import heapq

import jax
import jax.numpy as jnp
from jax import lax
from jax.experimental import pallas as pl
from jax.experimental.pallas import tpu as pltpu
from jax.sharding import PartitionSpec as P

F32 = jnp.float32
BF16 = jnp.bfloat16
BLK = 256
BASE = 16
MESH = pl.DeviceIdType.MESH
NX, NY, NZ = 4, 8, 8
COPIES = 320


def split(a):
    hi = a.astype(BF16)
    lo = (a - hi.astype(F32)).astype(BF16)
    return hi, lo


def dot(a, b, transposed=False):
    dims = (((1,), (1 if transposed else 0,)), ((), ()))
    return lax.dot_general(a, b, dims, preferred_element_type=F32)


def product(a, b):
    (ah, al), (bh, bl) = a, b
    return dot(ah, bh) + (dot(ah, bl) + dot(al, bh))


def thin_product(x, bh, bl, transposed=False):
    xh, xl = split(x)
    rows = x.shape[0]
    both = dot(jnp.concatenate([xh, xl], axis=0), bh, transposed)
    return both[:rows] + (both[rows:] + dot(xh, bl, transposed))


def unit_upper_inverses(mats):
    size = mats[0].shape[0]
    row = lax.broadcasted_iota(jnp.int32, (size, size), 0)
    col = lax.broadcasted_iota(jnp.int32, (size, size), 1)
    same = (row // BASE) == (col // BASE)
    eye = jnp.where(row == col, 1.0, 0.0)
    power = [jnp.where(same, -n, 0.0) for n in mats]
    inv = [eye + p for p in power]
    span = 2
    while span < BASE:
        parts = [split(p) for p in power]
        power = [product(p, p) for p in parts]
        parts = [split(p) for p in power]
        inv = [m + product(split(m), p) for m, p in zip(inv, parts)]
        span *= 2
        yield None
    width = BASE
    while width < size:
        corner = ((row // width) % 2 == 0) & ((col // width) == (row // width) + 1)
        parts = [split(m) for m in inv]
        corners = [product(split(jnp.where(corner, n, 0.0)), m) for n, m in zip(mats, parts)]
        inv = [m - product(ms, split(c)) for m, ms, c in zip(inv, parts, corners)]
        width *= 2
        yield None
    yield [split(m) for m in inv]


def ring_plan(n, kind):
    ahead, back = range(1, n // 2 + 1), range(1, n - n // 2)
    if kind == 0:
        step = {1: 0, 2: 1, 3: 2, 4: 3}
    elif kind == 1:
        step = {1: 0, 2: 0, 3: 2, 4: 2}
    parent = {e: step[e] for e in ahead}
    parent.update({-e: -step[e] for e in back})
    rank = {0: 0}
    for e in sorted(parent, key=abs):
        rank[e] = rank[parent[e]] + 1
    return parent, rank


def exchange_body(tri, couple, orb, diag, whole, diags, orbs, sent, first, diag_tile, diag_in, orb_in, local, send, recv, pack_work, invert, unpack):
    bulk, x = lax.axis_index("bulk"), lax.axis_index("rep")
    c = lax.rem(bulk, 2)
    z = lax.rem(bulk // 2, NZ)
    y = bulk // (2 * NZ)
    s = 1 - 2 * c
    me = {"x": x, "y": y, "z": z}
    size = {"x": NX, "y": NY, "z": NZ}
    used = {"send": 0, "recv": 0, "order": 0, "now": 0}

    def new(kind):
        used[kind] += 1
        return used[kind] - 1

    def shifted(axis, by):
        return lax.rem(me[axis] + by + 2 * size[axis], size[axis])

    def device(axis, by):
        at = dict(me)
        at[axis] = shifted(axis, by)
        return ((at["y"] * NZ + at["z"]) * 2 + c, at["x"])

    partner = (bulk + s, x)

    def put(src, dst, to, send_at, recv_at):
        pltpu.make_async_remote_copy(
            src_ref=src, dst_ref=dst, send_sem=send.at[send_at], recv_sem=recv.at[recv_at],
            device_id=to, device_id_type=MESH).start()

    def take(sem, ref):
        pltpu.make_async_copy(ref, ref, sem).wait()

    get_diag = pltpu.make_async_copy(diag, diag_in, local.at[0])
    get_orb = pltpu.make_async_copy(orb, orb_in, local.at[1])
    get_orb.start()
    get_diag.start()
    barrier = pltpu.get_barrier_semaphore()
    peers = [device(a, o) for a in "xyz" for o in range(1, size[a])] + [partner]
    for peer in peers:
        pl.semaphore_signal(barrier, inc=1, device_id=peer, device_id_type=MESH)
    keeps = []
    for t, ref in ((0, tri), (1, couple)):
        for half in range(2):
            keep = pltpu.make_async_copy(ref.at[:, pl.ds(128 * half, 128)], whole.at[t, half, x, y, z, c], local.at[2 + 2 * t + half])
            keep.start()
            keeps.append(keep)
    pl.semaphore_wait(barrier, len(peers))

    line_send = new("send")
    line_recv = {(t, half): new("recv") for t in range(2) for half in range(2)}
    order = (4, 3, 5, 2, 6, 1, 7)
    for o in order:
        for half, axis in ((0, "z"), (1, "y")):
            put(couple.at[:, pl.ds(128 * half, 128)], whole.at[1, half, x, y, z, c], device(axis, o), line_send, line_recv[1, half])
    for o in (2, 1, 3):
        for half in range(2):
            put(tri.at[:, pl.ds(128 * half, 128)], whole.at[0, half, x, y, z, c], device("x", o), line_send, line_recv[0, half])

    pack_work(get_orb, get_diag)
    put_diag = pltpu.make_async_copy(diag_tile, diags.at[y, z, c], local.at[6])
    put_diag.start()
    own_line = lax.select(c == 0, y, z)
    keep_first = pltpu.make_async_copy(sent.at[own_line], first.at[own_line], local.at[7])
    keep_first.start()
    diag_send, diag_recv = new("send"), new("recv")
    for o in order:
        put(diag_tile, diags.at[y, z, c], device("z", o), diag_send, diag_recv)

    colours = [(1, 0, "z", "y", "x"), (1, 1, "y", "z", "x"), (0, 0, "x", "z", "y"), (0, 1, "x", "y", "z")]
    ring_send = {colour: (new("send"), new("send")) for colour in colours}
    cross_send = new("send")
    cross_recv = {colour: new("recv") for colour in colours}

    def block(colour, index):
        t, half, line, _, _ = colour
        at = {**me, **index}
        at[line] = slice(None)
        return whole.at[t, half, at["x"], at["y"], at["z"], c]

    def tiles_like(n):
        for a in (4, 3, 2, 1):
            for b in range(8, 0, -1):
                if n % (a * b) == 0 and n // (a * b) <= 8:
                    return whole.at[0, 0, pl.ds(0, a), pl.ds(0, b), pl.ds(0, n // (a * b)), 0]

    events = []

    def later(time, action):
        heapq.heappush(events, (time, len(events) + used["order"], action))
        used["order"] += 1000

    crossings = []

    def to_partner(colour, ref):
        put(ref, ref, partner, cross_send, cross_recv[colour])
        crossings.append(colour)

    def final_ring(colour, indices, slot):
        axis = colour[4]
        kind = 0 if axis == "x" else 1
        parent, rank = ring_plan(size[axis], kind)
        sems = {e: new("recv") for e in parent}

        def pass_on(e):
            for index in indices:
                ref = block(colour, {**index, axis: shifted(axis, -s * e)})
                for f in parent:
                    if parent[f] == e and f != e:
                        put(ref, ref, device(axis, s * (f - e)), ring_send[colour][1], sems[f])
                to_partner(colour, ref)

        def action(e):
            take(recv.at[sems[e]], tiles_like(size[colour[2]] * len(indices)))
            pass_on(e)

        pass_on(0)
        for e in parent:
            if axis == "x":
                when = 20 + 40 * slot + 25 * rank[e]
            else:
                when = 5 + 30 * slot + 34 * rank[e]
            later(max(when, used["now"] + 1), functools.partial(action, e))

    def middle_ring(colour):
        axis = colour[3]
        parent, rank = ring_plan(size[axis], 0 if axis == "x" else 1)
        sems = {e: new("recv") for e in parent}

        def pass_on(e):
            ref = block(colour, {axis: shifted(axis, -s * e)})
            for f in parent:
                if parent[f] == e:
                    put(ref, ref, device(axis, s * (f - e)), ring_send[colour][0], sems[f])

        def action(es):
            for e in es:
                take(recv.at[sems[e]], tiles_like(size[colour[2]]))
                pass_on(e)
            indices = [{axis: shifted(axis, -s * e)} for e in es]
            final_ring(colour, indices, rank[es[0]])

        pass_on(0)
        for r in range(1, max(rank.values()) + 1):
            later((25 if colour[4] == "x" else 27) * r, functools.partial(action, [e for e in parent if rank[e] == r]))

    first_send, first_recv, second_send, second_recv = new("send"), new("recv"), new("send"), new("recv")
    dblock_send, dblock_recv = new("send"), new("recv")
    cross_small = [(new("send"), new("recv")) for _ in range(2)]

    one = lax.select(c == 0, y, z)
    two = lax.select(c == 0, z, y)

    def crossing_device(first_axis, by):
        along_y = lax.select(c == 0, by if first_axis else 0, 0 if first_axis else by)
        along_z = by - along_y
        at_y, at_z = lax.rem(y + along_y, NY), lax.rem(z + along_z, NZ)
        return ((at_y * NZ + at_z) * 2 + c, x)

    def orbital_first():
        for o in order:
            put(sent.at[lax.rem(one + o, 8)], first.at[one], crossing_device(True, o), first_send, first_recv)

    def orbital_second():
        keep_first.wait()
        take(recv.at[first_recv], first.at[pl.ds(0, 7)])
        keep_second = pltpu.make_async_copy(first.at[:, two], orbs.at[c, two], local.at[8])
        keep_second.start()
        for o in order:
            put(first.at[:, lax.rem(two + o, 8)], orbs.at[c, two], crossing_device(False, o), second_send, second_recv)
        keep_second.wait()

    def orbital_last():
        take(recv.at[second_recv], orbs.at[0, pl.ds(0, 7)])
        put(orbs.at[c], orbs.at[c], partner, *cross_small[0])

    def diag_second():
        put_diag.wait()
        take(recv.at[diag_recv], diags.at[0, pl.ds(0, 7), 0])
        for o in order:
            put(diags.at[y, :, c], diags.at[y, :, c], device("y", o), dblock_send, dblock_recv)

    def diag_last():
        take(recv.at[dblock_recv], diags.at[pl.ds(0, 7), :, 0])
        put(diags.at[:, :, c], diags.at[:, :, c], partner, *cross_small[1])

    for keep in keeps:
        keep.wait()
    orbital_first()
    for colour in colours:
        take(recv.at[line_recv[colour[0], colour[1]]], tiles_like(size[colour[2]] - 1))
        middle_ring(colour)
    for colour in colours[:2]:
        final_ring(colour, [{}], 0)
    for colour in colours[2:]:
        final_ring(colour, [{}], 0)

    later(45, orbital_second)
    later(110, orbital_last)
    later(40, diag_second)
    later(90, diag_last)

    def triangles_ready():
        take(recv.at[cross_small[1][1]], diags.at[:, :, 0])
        for colour in colours[2:]:
            take(recv.at[cross_recv[colour]], tiles_like(256))
        steps = invert()

        def advance():
            if next(steps, steps) is not steps:
                later(used["now"] + 1, advance)

        advance()

    def orbitals_ready():
        take(recv.at[cross_small[0][1]], orbs.at[0])
        unpack()

    later(134, triangles_ready)
    later(134 + 1, orbitals_ready)
    while events:
        time, _, action = heapq.heappop(events)
        used["now"] = time
        action()

    for colour in colours[:2]:
        take(recv.at[cross_recv[colour]], tiles_like(256))

    def finish():
        take(send.at[line_send], tiles_like(20))
        take(send.at[diag_send], diags.at[0, pl.ds(0, 7), 0])
        for colour in colours:
            per, middle, last = (size[axis] for axis in colour[2:])
            take(send.at[ring_send[colour][0]], tiles_like(per * (middle - 1)))
            take(send.at[ring_send[colour][1]], tiles_like(per * middle * (last - 1)))
        take(send.at[cross_send], whole.at[:, :, :, :, :, 0])
        take(send.at[first_send], first.at[pl.ds(0, 7)])
        take(send.at[second_send], orbs.at[0, pl.ds(0, 7)])
        take(send.at[dblock_send], diags.at[pl.ds(0, 7), :, 0])
        take(send.at[cross_small[0][0]], orbs.at[0])
        take(send.at[cross_small[1][0]], diags.at[:, :, 0])

    assert used["send"] <= SENDS and used["recv"] <= RECVS
    return finish


def pack_into(orb_in, diag_in, sent, diag_tile):
    place = lax.axis_index("bulk") % 16
    odd = lax.axis_index("bulk") % 2 == 1
    lane = lax.broadcasted_iota(jnp.int32, (2, 128), 1)
    spread = jnp.concatenate([diag_in[...]] * 16, axis=1)
    diag_tile[...] = jnp.where(lane // 8 == place, spread, 0.0)
    group = lax.broadcasted_iota(jnp.int32, (8, 128), 1) // 16
    for g in range(4):
        stack = jnp.concatenate([orb_in[:, pl.ds(128 * (8 * g + t), 128)] for t in range(8)], axis=0)
        turned = stack.T
        for p in range(2):
            pieces = [turned[64 * p + 8 * h : 64 * p + 8 * h + 8] for h in range(8)]
            for t in range(8):
                tile = jnp.zeros((8, 128), F32)
                for h in range(8):
                    moved = pieces[h] if h == t else pltpu.roll(pieces[h], (16 * (h - t)) % 128, 1)
                    tile = jnp.where(group == h, moved, tile)
                chip = 2 * (8 * g + t) + p
                sent[lax.select(odd, chip % NZ, chip // NZ), lax.select(odd, chip // NZ, chip % NZ)] = tile


def exchange_kernel(tri, couple, orb, diag, out_ref, whole, diags, orbs, sent, first, diag_tile, diag_in, orb_in, mh_ref, ml_ref, local, send, recv):
    def pack_work(get_orb, get_diag):
        get_diag.wait()
        get_orb.wait()
        pack_into(orb_in, diag_in, sent, diag_tile)

    panel = 1024
    count = panel // BLK
    row = lax.broadcasted_iota(jnp.int32, (BLK, BLK), 0)
    col = lax.broadcasted_iota(jnp.int32, (BLK, BLK), 1)
    upper = row < col

    def factor(t, i, j):
        return jnp.concatenate([whole[t, half, i, 2 * j : 2 * j + 2].reshape(BLK, 128) for half in range(2)], axis=1)

    state = {}

    def invert():
        scales = []
        for which in range(2):
            rows = [jnp.sum(diags[w, :, :, which, :].reshape(16, 128), axis=0, keepdims=True) for w in range(8)]
            scales.append([1.0 / jnp.concatenate(rows[2 * k : 2 * k + 2], axis=1) for k in range(count)])

        half = BLK // 2
        above = upper[:half, :half]
        mats, corners = [], []
        for k in range(count):
            block = factor(0, k, k)
            for which, turned in ((0, block), (1, block.T)):
                scaled = turned * scales[which][k]
                mats += [jnp.where(above, scaled[:half, :half], 0.0), jnp.where(above, scaled[half:, half:], 0.0)]
                corners.append(scaled[:half, half:])
        for invs in unit_upper_inverses(mats):
            yield
        inner = [product(split(n), invs[2 * e + 1]) for e, n in enumerate(corners)]
        inner = [split(-product(invs[2 * e], split(n))) for e, n in enumerate(inner)]
        for k in range(count):
            for which in range(2):
                e = 2 * k + which
                for at, ref in enumerate((mh_ref, ml_ref)):
                    ref[which, k, :half, :half] = invs[2 * e][at]
                    ref[which, k, half:, half:] = invs[2 * e + 1][at]
                    ref[which, k, :half, half:] = inner[e][at]
                    ref[which, k, half:, :half] = jnp.zeros((half, half), BF16)

        state["scales"] = scales

    def unpack():
        odd = lax.axis_index("bulk") % 2 == 1
        group = lax.broadcasted_iota(jnp.int32, (8, 128), 1) // 16
        columns = []
        for w in range(16):
            places = [(4 * (w % 2) + e // 2, w // 2) for e in range(8)]
            tiles = [orbs[1, py, pz] if e % 2 else orbs[0, pz, py] for e, (pz, py) in enumerate(places)]
            tiles = [jnp.where(odd, pltpu.roll(t, 64, 1), t) for t in tiles]
            strips = []
            for h in range(4):
                strip = jnp.zeros((8, 128), F32)
                for e in range(8):
                    moved = tiles[e] if e == h else pltpu.roll(tiles[e], (16 * (e - h)) % 128, 1)
                    strip = jnp.where(group == e, moved, strip)
                strips.append(strip)
            columns.append(jnp.concatenate(strips, axis=0))
        blocks = [jnp.concatenate(columns[2 * k : 2 * k + 2], axis=1) for k in range(2 * count)]
        left, right = blocks[:count], blocks[count:]
        state["columns"] = left, right

    finish = exchange_body(tri, couple, orb, diag, whole, diags, orbs, sent, first, diag_tile, diag_in, orb_in, local, send, recv, pack_work, invert, unpack)
    scales = state["scales"]
    left, right = state["columns"]
    for k in range(count):
        x = thin_product(left[k] * scales[0][k], mh_ref[0, k], ml_ref[0, k])
        out_ref[:, pl.ds(BLK * k, BLK)] = x
        for i in range(k + 1, count):
            left[i] = left[i] - thin_product(x, *split(factor(0, i, k)))
        for i in range(count):
            right[i] = right[i] - thin_product(x, *split(factor(1, i, k)))
    for k in range(count):
        x = thin_product(right[k] * scales[1][k], mh_ref[1, k], ml_ref[1, k])
        out_ref[:, pl.ds(panel + BLK * k, BLK)] = x
        for i in range(k + 1, count):
            right[i] = right[i] - thin_product(x, *split(factor(0, k, i)), transposed=True)


    finish()


SENDS, RECVS = 24, 112


def exchange(orbitals, triangles, coupling, diagonals):
    anywhere = pl.BlockSpec(memory_space=pl.ANY)
    vmem = pl.BlockSpec(memory_space=pltpu.VMEM)
    return pl.pallas_call(
        exchange_kernel,
        out_shape=jax.ShapeDtypeStruct((32, 2048), F32),
        in_specs=[anywhere] * 4,
        out_specs=vmem,
        scratch_shapes=[
            pltpu.VMEM((2, 2, NX, NY, NZ, 2, 8, 128), F32),
            pltpu.VMEM((NY, NZ, 2, 2, 128), F32),
            pltpu.VMEM((2, NZ, NY, 8, 128), F32),
            pltpu.VMEM((NY, NZ, 8, 128), F32),
            pltpu.VMEM((NY, NZ, 8, 128), F32),
            pltpu.VMEM((2, 128), F32),
            pltpu.VMEM((2, 8), F32),
            pltpu.VMEM((16, 4096), F32),
            pltpu.VMEM((2, 4, BLK, BLK), BF16),
            pltpu.VMEM((2, 4, BLK, BLK), BF16),
            pltpu.SemaphoreType.DMA((9,)),
            pltpu.SemaphoreType.DMA((SENDS,)),
            pltpu.SemaphoreType.DMA((RECVS,)),
        ],
        compiler_params=pltpu.CompilerParams(collective_id=0, has_side_effects=True, vmem_limit_bytes=62 << 20),
        name="exchange",
    )(triangles, coupling, orbitals, diagonals)


def per_device(orbitals, triangles, coupling, diagonals):
    return exchange(orbitals.T, triangles.T, coupling.T, diagonals)


def solution(mesh):
    return jax.shard_map(
        per_device,
        mesh=mesh,
        in_specs=(P("rep", "bulk"), P("rep", "bulk"), P("rep", "bulk"), P(None, "bulk")),
        out_specs=P(("rep", "bulk"), None),
        check_vma=False,
    )
```

```python
import functools
import heapq

import jax
import jax.numpy as jnp
from jax import lax
from jax.experimental import pallas as pl
from jax.experimental.pallas import tpu as pltpu
from jax.sharding import PartitionSpec as P

F32 = jnp.float32
BF16 = jnp.bfloat16
BLK = 256
BASE = 16
MESH = pl.DeviceIdType.MESH
NX, NY, NZ = 4, 8, 8
COPIES = 320


def split(a):
    hi = a.astype(BF16)
    lo = (a - hi.astype(F32)).astype(BF16)
    return hi, lo


def dot(a, b, transposed=False):
    dims = (((1,), (1 if transposed else 0,)), ((), ()))
    return lax.dot_general(a, b, dims, preferred_element_type=F32)


def product(a, b):
    (ah, al), (bh, bl) = a, b
    return dot(ah, bh) + (dot(ah, bl) + dot(al, bh))


def thin_product(x, bh, bl, transposed=False):
    xh, xl = split(x)
    rows = x.shape[0]
    both = dot(jnp.concatenate([xh, xl], axis=0), bh, transposed)
    return both[:rows] + (both[rows:] + dot(xh, bl, transposed))


def unit_upper_inverses(mats):
    size = mats[0].shape[0]
    row = lax.broadcasted_iota(jnp.int32, (size, size), 0)
    col = lax.broadcasted_iota(jnp.int32, (size, size), 1)
    same = (row // BASE) == (col // BASE)
    eye = jnp.where(row == col, 1.0, 0.0)
    power = [jnp.where(same, -n, 0.0) for n in mats]
    inv = [eye + p for p in power]
    span = 2
    while span < BASE:
        parts = [split(p) for p in power]
        power = [product(p, p) for p in parts]
        parts = [split(p) for p in power]
        inv = [m + product(split(m), p) for m, p in zip(inv, parts)]
        span *= 2
        yield None
    width = BASE
    while width < size:
        corner = ((row // width) % 2 == 0) & ((col // width) == (row // width) + 1)
        parts = [split(m) for m in inv]
        corners = [product(split(jnp.where(corner, n, 0.0)), m) for n, m in zip(mats, parts)]
        inv = [m - product(ms, split(c)) for m, ms, c in zip(inv, parts, corners)]
        width *= 2
        yield None
    yield [split(m) for m in inv]


def ring_plan(n, kind):
    ahead, back = range(1, n // 2 + 1), range(1, n - n // 2)
    if kind == 0:
        step = {1: 0, 2: 1, 3: 2, 4: 3}
    elif kind == 1:
        step = {1: 0, 2: 0, 3: 2, 4: 2}
    parent = {e: step[e] for e in ahead}
    parent.update({-e: -step[e] for e in back})
    rank = {0: 0}
    for e in sorted(parent, key=abs):
        rank[e] = rank[parent[e]] + 1
    return parent, rank


def exchange_body(tri, couple, orb, diag, whole, diags, orbs, sent, first, diag_tile, diag_in, orb_in, local, send, recv, pack_work, invert, unpack, solve_left, subtract):
    bulk, x = lax.axis_index("bulk"), lax.axis_index("rep")
    c = lax.rem(bulk, 2)
    z = lax.rem(bulk // 2, NZ)
    y = bulk // (2 * NZ)
    s = 1 - 2 * c
    me = {"x": x, "y": y, "z": z}
    size = {"x": NX, "y": NY, "z": NZ}
    used = {"send": 0, "recv": 0, "order": 0, "now": 0}

    def new(kind):
        used[kind] += 1
        return used[kind] - 1

    def shifted(axis, by):
        return lax.rem(me[axis] + by + 2 * size[axis], size[axis])

    def device(axis, by):
        at = dict(me)
        at[axis] = shifted(axis, by)
        return ((at["y"] * NZ + at["z"]) * 2 + c, at["x"])

    partner = (bulk + s, x)

    def put(src, dst, to, send_at, recv_at):
        pltpu.make_async_remote_copy(
            src_ref=src, dst_ref=dst, send_sem=send.at[send_at], recv_sem=recv.at[recv_at],
            device_id=to, device_id_type=MESH).start()

    def take(sem, ref):
        pltpu.make_async_copy(ref, ref, sem).wait()

    get_diag = pltpu.make_async_copy(diag, diag_in, local.at[0])
    get_orb = pltpu.make_async_copy(orb, orb_in, local.at[1])
    get_orb.start()
    get_diag.start()
    barrier = pltpu.get_barrier_semaphore()
    peers = [device(a, o) for a in "xyz" for o in range(1, size[a])] + [partner]
    for peer in peers:
        pl.semaphore_signal(barrier, inc=1, device_id=peer, device_id_type=MESH)
    keeps = []
    for t, ref in ((0, tri), (1, couple)):
        for half in range(2):
            keep = pltpu.make_async_copy(ref.at[:, pl.ds(128 * half, 128)], whole.at[t, half, x, y, z, c], local.at[2 + 2 * t + half])
            keep.start()
            keeps.append(keep)
    pl.semaphore_wait(barrier, len(peers))

    line_send = new("send")
    line_recv = {(t, half): new("recv") for t in range(2) for half in range(2)}
    order = (4, 3, 5, 2, 6, 1, 7)
    for o in order:
        for half, axis in ((0, "z"), (1, "y")):
            put(couple.at[:, pl.ds(128 * half, 128)], whole.at[1, half, x, y, z, c], device(axis, o), line_send, line_recv[1, half])
    for o in (2, 1, 3):
        for half in range(2):
            put(tri.at[:, pl.ds(128 * half, 128)], whole.at[0, half, x, y, z, c], device("x", o), line_send, line_recv[0, half])

    pack_work(get_orb, get_diag)
    put_diag = pltpu.make_async_copy(diag_tile, diags.at[y, z, c], local.at[6])
    put_diag.start()
    own_line = lax.select(c == 0, y, z)
    keep_first = pltpu.make_async_copy(sent.at[own_line], first.at[own_line], local.at[7])
    keep_first.start()
    diag_send, diag_recv = new("send"), new("recv")
    for o in order:
        put(diag_tile, diags.at[y, z, c], device("z", o), diag_send, diag_recv)

    colours = [(1, 0, "z", "y", "x"), (1, 1, "y", "z", "x"), (0, 0, "x", "z", "y"), (0, 1, "x", "y", "z")]
    ring_send = {colour: (new("send"), new("send")) for colour in colours}
    cross_send = new("send")
    cross_recv = {colour: new("recv") for colour in colours}

    def block(colour, index):
        t, half, line, _, _ = colour
        at = {**me, **index}
        at[line] = slice(None)
        return whole.at[t, half, at["x"], at["y"], at["z"], c]

    def tiles_like(n):
        for a in (4, 3, 2, 1):
            for b in range(8, 0, -1):
                if n % (a * b) == 0 and n // (a * b) <= 8:
                    return whole.at[0, 0, pl.ds(0, a), pl.ds(0, b), pl.ds(0, n // (a * b)), 0]

    events = []

    def later(time, action):
        heapq.heappush(events, (time, len(events) + used["order"], action))
        used["order"] += 1000

    crossings = []

    def to_partner(colour, ref):
        put(ref, ref, partner, cross_send, cross_recv[colour])
        crossings.append(colour)

    def final_ring(colour, indices, slot):
        axis = colour[4]
        kind = 0 if axis == "x" else 1
        parent, rank = ring_plan(size[axis], kind)
        sems = {e: new("recv") for e in parent}

        def pass_on(e):
            for index in indices:
                ref = block(colour, {**index, axis: shifted(axis, -s * e)})
                for f in parent:
                    if parent[f] == e and f != e:
                        put(ref, ref, device(axis, s * (f - e)), ring_send[colour][1], sems[f])
                to_partner(colour, ref)

        def action(e):
            take(recv.at[sems[e]], tiles_like(size[colour[2]] * len(indices)))
            pass_on(e)

        pass_on(0)
        for e in parent:
            if axis == "x":
                when = 20 + 40 * slot + 25 * rank[e]
            else:
                when = 5 + 30 * slot + 34 * rank[e]
            later(max(when, used["now"] + 1), functools.partial(action, e))

    def middle_ring(colour):
        axis = colour[3]
        parent, rank = ring_plan(size[axis], 0 if axis == "x" else 1)
        sems = {e: new("recv") for e in parent}

        def pass_on(e):
            ref = block(colour, {axis: shifted(axis, -s * e)})
            for f in parent:
                if parent[f] == e:
                    put(ref, ref, device(axis, s * (f - e)), ring_send[colour][0], sems[f])

        def action(es):
            for e in es:
                take(recv.at[sems[e]], tiles_like(size[colour[2]]))
                pass_on(e)
            indices = [{axis: shifted(axis, -s * e)} for e in es]
            final_ring(colour, indices, rank[es[0]])

        pass_on(0)
        for r in range(1, max(rank.values()) + 1):
            later((25 if colour[4] == "x" else 27) * r, functools.partial(action, [e for e in parent if rank[e] == r]))

    first_send, first_recv, second_send, second_recv = new("send"), new("recv"), new("send"), new("recv")
    dblock_send, dblock_recv = new("send"), new("recv")
    cross_small = [(new("send"), new("recv")) for _ in range(2)]

    one = lax.select(c == 0, y, z)
    two = lax.select(c == 0, z, y)

    def crossing_device(first_axis, by):
        along_y = lax.select(c == 0, by if first_axis else 0, 0 if first_axis else by)
        along_z = by - along_y
        at_y, at_z = lax.rem(y + along_y, NY), lax.rem(z + along_z, NZ)
        return ((at_y * NZ + at_z) * 2 + c, x)

    def orbital_first():
        for o in order:
            put(sent.at[lax.rem(one + o, 8)], first.at[one], crossing_device(True, o), first_send, first_recv)

    def orbital_second():
        keep_first.wait()
        take(recv.at[first_recv], first.at[pl.ds(0, 7)])
        keep_second = pltpu.make_async_copy(first.at[:, two], orbs.at[c, two], local.at[8])
        keep_second.start()
        for o in order:
            put(first.at[:, lax.rem(two + o, 8)], orbs.at[c, two], crossing_device(False, o), second_send, second_recv)
        keep_second.wait()

    def orbital_last():
        take(recv.at[second_recv], orbs.at[0, pl.ds(0, 7)])
        put(orbs.at[c], orbs.at[c], partner, *cross_small[0])

    def diag_second():
        put_diag.wait()
        take(recv.at[diag_recv], diags.at[0, pl.ds(0, 7), 0])
        for o in order:
            put(diags.at[y, :, c], diags.at[y, :, c], device("y", o), dblock_send, dblock_recv)

    def diag_last():
        take(recv.at[dblock_recv], diags.at[pl.ds(0, 7), :, 0])
        put(diags.at[:, :, c], diags.at[:, :, c], partner, *cross_small[1])

    for keep in keeps:
        keep.wait()
    orbital_first()
    for colour in colours:
        take(recv.at[line_recv[colour[0], colour[1]]], tiles_like(size[colour[2]] - 1))
        middle_ring(colour)
    for colour in colours[:2]:
        final_ring(colour, [{}], 0)
    for colour in colours[2:]:
        final_ring(colour, [{}], 0)

    later(45, orbital_second)
    later(110, orbital_last)
    later(40, diag_second)
    later(90, diag_last)

    def triangles_ready():
        take(recv.at[cross_small[1][1]], diags.at[:, :, 0])
        for colour in colours[2:]:
            take(recv.at[cross_recv[colour]], tiles_like(256))
        steps = invert()

        def advance():
            if next(steps, steps) is not steps:
                later(used["now"] + 1, advance)

        advance()

    def orbitals_ready():
        take(recv.at[cross_small[0][1]], orbs.at[0])
        unpack()

    later(134, triangles_ready)
    later(136, orbitals_ready)
    while events:
        time, _, action = heapq.heappop(events)
        used["now"] = time
        action()

    solve_left()
    for colour in colours[:2]:
        take(recv.at[cross_recv[colour]], tiles_like(256))
        subtract(colour[1])

    def finish():
        take(send.at[line_send], tiles_like(20))
        take(send.at[diag_send], diags.at[0, pl.ds(0, 7), 0])
        for colour in colours:
            per, middle, last = (size[axis] for axis in colour[2:])
            take(send.at[ring_send[colour][0]], tiles_like(per * (middle - 1)))
            take(send.at[ring_send[colour][1]], tiles_like(per * middle * (last - 1)))
        take(send.at[cross_send], whole.at[:, :, :, :, :, 0])
        take(send.at[first_send], first.at[pl.ds(0, 7)])
        take(send.at[second_send], orbs.at[0, pl.ds(0, 7)])
        take(send.at[dblock_send], diags.at[pl.ds(0, 7), :, 0])
        take(send.at[cross_small[0][0]], orbs.at[0])
        take(send.at[cross_small[1][0]], diags.at[:, :, 0])

    assert used["send"] <= SENDS and used["recv"] <= RECVS
    return finish


def pack_into(orb_in, diag_in, sent, diag_tile):
    place = lax.axis_index("bulk") % 16
    odd = lax.axis_index("bulk") % 2 == 1
    lane = lax.broadcasted_iota(jnp.int32, (2, 128), 1)
    spread = jnp.concatenate([diag_in[...]] * 16, axis=1)
    diag_tile[...] = jnp.where(lane // 8 == place, spread, 0.0)
    group = lax.broadcasted_iota(jnp.int32, (8, 128), 1) // 16
    for g in range(4):
        stack = jnp.concatenate([orb_in[:, pl.ds(128 * (8 * g + t), 128)] for t in range(8)], axis=0)
        turned = stack.T
        for p in range(2):
            pieces = [turned[64 * p + 8 * h : 64 * p + 8 * h + 8] for h in range(8)]
            for t in range(8):
                tile = jnp.zeros((8, 128), F32)
                for h in range(8):
                    moved = pieces[h] if h == t else pltpu.roll(pieces[h], (16 * (h - t)) % 128, 1)
                    tile = jnp.where(group == h, moved, tile)
                chip = 2 * (8 * g + t) + p
                sent[lax.select(odd, chip % NZ, chip // NZ), lax.select(odd, chip // NZ, chip % NZ)] = tile


def exchange_kernel(tri, couple, orb, diag, out_ref, whole, diags, orbs, sent, first, diag_tile, diag_in, orb_in, mh_ref, ml_ref, local, send, recv):
    def pack_work(get_orb, get_diag):
        get_diag.wait()
        get_orb.wait()
        pack_into(orb_in, diag_in, sent, diag_tile)

    panel = 1024
    count = panel // BLK
    row = lax.broadcasted_iota(jnp.int32, (BLK, BLK), 0)
    col = lax.broadcasted_iota(jnp.int32, (BLK, BLK), 1)
    upper = row < col

    def factor(t, i, j):
        return jnp.concatenate([whole[t, half, i, 2 * j : 2 * j + 2].reshape(BLK, 128) for half in range(2)], axis=1)

    state = {}

    def invert():
        scales = []
        for which in range(2):
            rows = [jnp.sum(diags[w, :, :, which, :].reshape(16, 128), axis=0, keepdims=True) for w in range(8)]
            scales.append([1.0 / jnp.concatenate(rows[2 * k : 2 * k + 2], axis=1) for k in range(count)])

        half = BLK // 2
        above = upper[:half, :half]
        mats, corners = [], []
        for k in range(count):
            block = factor(0, k, k)
            for which, turned in ((0, block), (1, block.T)):
                scaled = turned * scales[which][k]
                mats += [jnp.where(above, scaled[:half, :half], 0.0), jnp.where(above, scaled[half:, half:], 0.0)]
                corners.append(scaled[:half, half:])
        for invs in unit_upper_inverses(mats):
            yield
        inner = [product(split(n), invs[2 * e + 1]) for e, n in enumerate(corners)]
        inner = [split(-product(invs[2 * e], split(n))) for e, n in enumerate(inner)]
        for k in range(count):
            for which in range(2):
                e = 2 * k + which
                for at, ref in enumerate((mh_ref, ml_ref)):
                    ref[which, k, :half, :half] = invs[2 * e][at]
                    ref[which, k, half:, half:] = invs[2 * e + 1][at]
                    ref[which, k, :half, half:] = inner[e][at]
                    ref[which, k, half:, :half] = jnp.zeros((half, half), BF16)

        state["scales"] = scales

    def unpack():
        odd = lax.axis_index("bulk") % 2 == 1
        group = lax.broadcasted_iota(jnp.int32, (8, 128), 1) // 16
        columns = []
        for w in range(16):
            places = [(4 * (w % 2) + e // 2, w // 2) for e in range(8)]
            tiles = [orbs[1, py, pz] if e % 2 else orbs[0, pz, py] for e, (pz, py) in enumerate(places)]
            tiles = [jnp.where(odd, pltpu.roll(t, 64, 1), t) for t in tiles]
            strips = []
            for h in range(4):
                strip = jnp.zeros((8, 128), F32)
                for e in range(8):
                    moved = tiles[e] if e == h else pltpu.roll(tiles[e], (16 * (e - h)) % 128, 1)
                    strip = jnp.where(group == e, moved, strip)
                strips.append(strip)
            columns.append(jnp.concatenate(strips, axis=0))
        blocks = [jnp.concatenate(columns[2 * k : 2 * k + 2], axis=1) for k in range(2 * count)]
        left, right = blocks[:count], blocks[count:]
        state["columns"] = left, right

    def solve_left():
        scales = state["scales"]
        left, _ = state["columns"]
        solved = []
        for k in range(count):
            x = thin_product(left[k] * scales[0][k], mh_ref[0, k], ml_ref[0, k])
            out_ref[:, pl.ds(BLK * k, BLK)] = x
            solved.append(x)
            for i in range(k + 1, count):
                left[i] = left[i] - thin_product(x, *split(factor(0, i, k)))
        state["solved"] = jnp.concatenate(solved, axis=1)
        state["updates"] = {}

    def subtract(half):
        for pair in range(count // 2):
            both = jnp.concatenate([whole[1, half, 2 * pair + e].reshape(panel, 128) for e in range(2)], axis=1)
            update = thin_product(state["solved"], *split(both))
            for e in range(2):
                state["updates"][half, 2 * pair + e] = update[:, 128 * e : 128 * e + 128]

    finish = exchange_body(tri, couple, orb, diag, whole, diags, orbs, sent, first, diag_tile, diag_in, orb_in, local, send, recv, pack_work, invert, unpack, solve_left, subtract)
    scales = state["scales"]
    _, right = state["columns"]
    updates = state["updates"]
    right = [right[i] - jnp.concatenate([updates[0, i], updates[1, i]], axis=1) for i in range(count)]
    for k in range(count):
        x = thin_product(right[k] * scales[1][k], mh_ref[1, k], ml_ref[1, k])
        out_ref[:, pl.ds(panel + BLK * k, BLK)] = x
        for i in range(k + 1, count):
            right[i] = right[i] - thin_product(x, *split(factor(0, k, i)), transposed=True)


    finish()


SENDS, RECVS = 24, 112


def exchange(orbitals, triangles, coupling, diagonals):
    anywhere = pl.BlockSpec(memory_space=pl.ANY)
    vmem = pl.BlockSpec(memory_space=pltpu.VMEM)
    return pl.pallas_call(
        exchange_kernel,
        out_shape=jax.ShapeDtypeStruct((32, 2048), F32),
        in_specs=[anywhere] * 4,
        out_specs=vmem,
        scratch_shapes=[
            pltpu.VMEM((2, 2, NX, NY, NZ, 2, 8, 128), F32),
            pltpu.VMEM((NY, NZ, 2, 2, 128), F32),
            pltpu.VMEM((2, NZ, NY, 8, 128), F32),
            pltpu.VMEM((NY, NZ, 8, 128), F32),
            pltpu.VMEM((NY, NZ, 8, 128), F32),
            pltpu.VMEM((2, 128), F32),
            pltpu.VMEM((2, 8), F32),
            pltpu.VMEM((16, 4096), F32),
            pltpu.VMEM((2, 4, BLK, BLK), BF16),
            pltpu.VMEM((2, 4, BLK, BLK), BF16),
            pltpu.SemaphoreType.DMA((9,)),
            pltpu.SemaphoreType.DMA((SENDS,)),
            pltpu.SemaphoreType.DMA((RECVS,)),
        ],
        compiler_params=pltpu.CompilerParams(collective_id=0, has_side_effects=True, vmem_limit_bytes=62 << 20),
        name="exchange",
    )(triangles, coupling, orbitals, diagonals)


def per_device(orbitals, triangles, coupling, diagonals):
    return exchange(orbitals.T, triangles.T, coupling.T, diagonals)


def solution(mesh):
    return jax.shard_map(
        per_device,
        mesh=mesh,
        in_specs=(P("rep", "bulk"), P("rep", "bulk"), P("rep", "bulk"), P(None, "bulk")),
        out_specs=P(("rep", "bulk"), None),
        check_vma=False,
    )
```
